256 devices in a mesh: lat: 16 (over y_hi, z), lon: 8 (over y_lo, x), head: 2 (over core).
Axes of the slice: x: 4, y: 4 (y_hi: 2, y_lo: 2; y = y_hi * 2 + y_lo), z: 8, core: 2. Of those that a mesh axis runs over, the one named last changes fastest.
Arguments:
- queries: bfloat16 [16, 8, 512, 1024], P('lat', 'lon', None, 'head'), may hold values from -250 to 250, as said below
- key_value: bfloat16 [16, 8, 512, 128], P('lat', 'lon'), may hold values from -5 to 5
- dout: bfloat16 [16, 8, 512, 1024], P('lat', 'lon', None, 'head'), may hold values from -6 to 6
Outputs:
- dquery: bfloat16 [16, 8, 512, 1024], P('lat', 'lon', None, 'head')
- dkey_value: float32 [16, 8, 512, 128], P('lat', 'lon', 'head')
The draws below stay inside these ranges and needn't reach their ends.
Inputs may be any that keep to these rules, and one draw needn't show every extreme that they name: `queries`: queries and keys have entries of order one, except that some query rows may be large multiples of nearby keys.
All inputs are finite; a program needn't handle non-finite values.
Results may differ from the reference program's by a relative error of at most 0.005.
Values may be sent and summed in bfloat16 or wider, within the bound.
No kernel may reach another device: no remote copies, remote signals or barrier semaphores. Data moves between devices by JAX's collectives and lax.ppermute only.
A program may use at most 64 MiB of HBM per device.

```python
import jax
import jax.numpy as jnp
from jax import lax

HEADS = 16
HEAD_DIM = 64
TOK = 512
NLAT = 16
NLON = 8


def joint_draw(key):
    base = jax.random.fold_in(key, 11)
    first, second = jax.random.split(base, 2)
    pairs = jnp.clip(jax.random.normal(first, (NLAT, NLON, TOK, 2 * HEAD_DIM), jnp.float32), -5.0, 5.0)
    query_full = jnp.clip(jax.random.normal(second, (NLAT, NLON, TOK, HEADS, HEAD_DIM), jnp.float32), -5.0, 5.0)
    return (query_full.reshape(NLAT, NLON, TOK, HEADS * HEAD_DIM), pairs)


def draw_queries(key, part):
    return joint_draw(key)[0].astype(jnp.bfloat16)


def draw_key_value(key, part):
    return joint_draw(key)[1].astype(jnp.bfloat16)


def steps_of(own_key, dims, pieces, least, high):
    loudness = 1.0
    for dim, shards_of in pieces:
        draws = jax.random.uniform(jax.random.fold_in(jax.random.fold_in(own_key, 6), dim), (shards_of,), jnp.float32, least / len(pieces), high / len(pieces))
        loudness = loudness * jnp.repeat(jnp.exp(draws), dims[dim] // shards_of).reshape((-1,) + (1,) * (len(dims) - 1 - dim))
    return loudness


def gaussian(own_key, extent, width, limit, cuts=(), held_as=jnp.bfloat16):
    values = jax.random.normal(own_key, extent, jnp.float32) * width
    if len(cuts) > 0:
        values = steps_of(own_key, extent, cuts, -0.22, 0.18) * values
    return jnp.clip(values, min=-limit, max=limit).astype(held_as)


def setup_inputs(seed: int = 0) -> dict:
    streams_of = jax.random.split(jax.random.key(seed), 4)
    queries = draw_queries(jax.random.fold_in(streams_of[3], 71), 0)
    key_value = draw_key_value(jax.random.fold_in(streams_of[3], 71), 0)
    dout = gaussian(streams_of[2], (NLAT, NLON, TOK, HEADS * HEAD_DIM), 1.0, 6.0, ((0, 16), (1, 8), (3, 2)))
    return {"queries": queries, "key_value": key_value, "dout": dout}


def tile_grads(operands):
    query_tile, dout_tile, keys_tile = operands
    tokens = query_tile.shape[0]
    scale = 1.0 / (HEAD_DIM ** 0.5)
    q_heads = query_tile.reshape(tokens, HEADS, HEAD_DIM).astype(jnp.float32)
    d_heads = dout_tile.reshape(tokens, HEADS, HEAD_DIM).astype(jnp.float32)
    keys = keys_tile[:, :HEAD_DIM].astype(jnp.float32)
    values = keys_tile[:, HEAD_DIM:].astype(jnp.float32)
    scores = jnp.einsum("thd,kd->htk", q_heads, keys) * scale
    top = jnp.max(scores, axis=-1, keepdims=True)
    expo = jnp.exp(scores - top)
    probs = expo / jnp.sum(expo, axis=-1, keepdims=True)
    probs_low = lax.optimization_barrier(probs.astype(jnp.bfloat16)).astype(jnp.float32)
    dprobs = jnp.einsum("thd,kd->htk", d_heads, values)
    delta = jnp.sum(probs * dprobs, axis=-1, keepdims=True)
    dscore = lax.optimization_barrier((probs * (dprobs - delta) * scale).astype(jnp.bfloat16)).astype(jnp.float32)
    dquery = jnp.einsum("htk,kd->thd", dscore, keys).astype(jnp.bfloat16).reshape(tokens, HEADS * HEAD_DIM)
    dkeys = jnp.einsum("htk,thd->kd", dscore, q_heads)
    dvalues = jnp.einsum("htk,thd->kd", probs_low, d_heads)
    return dquery, jnp.concatenate([dkeys, dvalues], axis=1)


def reference(queries, key_value, dout):
    tiles = NLAT * NLON
    near = jnp.stack([key_value, jnp.roll(key_value, -2, 0), jnp.roll(key_value, 2, 0), jnp.roll(key_value, -2, 1), jnp.roll(key_value, 2, 1)], axis=2)
    near = near.reshape(tiles, 5 * TOK, 2 * HEAD_DIM)
    dquery, contrib = lax.map(tile_grads, (queries.reshape(tiles, TOK, HEADS * HEAD_DIM), dout.reshape(tiles, TOK, HEADS * HEAD_DIM), near))
    dquery = dquery.reshape(NLAT, NLON, TOK, HEADS * HEAD_DIM)
    contrib = contrib.reshape(NLAT, NLON, 5, TOK, 2 * HEAD_DIM)
    total = contrib[:, :, 0]
    total = total + jnp.roll(contrib[:, :, 1], 2, 0)
    total = total + jnp.roll(contrib[:, :, 2], -2, 0)
    total = total + jnp.roll(contrib[:, :, 3], 2, 1)
    total = total + jnp.roll(contrib[:, :, 4], -2, 1)
    return dquery, total
```

```python
import functools

import jax
import jax.numpy as jnp
from jax import lax
from jax.experimental import pallas as pl
from jax.experimental.pallas import tpu as pltpu
from jax.sharding import PartitionSpec as P
HD=64
CH=256
def kernel(heads, tok, tiles, q_ref, d_ref, *rest):
    kv_refs=rest[:tiles]; dq_ref, g_ref = rest[tiles:tiles+2]
    qz, dz, kT, s_ref, dp_ref, e_ref, acc, dqt, w_ref, stat = rest[tiles+2:]
    per=tok//CH; nch=tiles*per
    scale=1.0/HD**0.5
    c2=1.4426950408889634*scale
    f32=jnp.float32; bf=jnp.bfloat16
    def kvc(c): return kv_refs[c//per][(c%per)*CH:(c%per+1)*CH,:]
    zero=jnp.zeros((HD,tok),bf)
    qT=q_ref[...].T; dT=d_ref[...].T
    for h in range(heads):
        qz[h,:HD,:]=qT[h*HD:(h+1)*HD,:]; qz[h,HD:,:]=zero
        dz[h,HD:,:]=dT[h*HD:(h+1)*HD,:]; dz[h,:HD,:]=zero
    for c in range(nch):
        kT[:,c*CH:(c+1)*CH]=kvc(c).T[:HD,:]
        acc[c]=jnp.zeros((CH,2*HD),f32)
    def g8(x): return x.reshape(CH//8,8,tok)
    def allmax(x):
        return jnp.broadcast_to(jnp.max(x,axis=0,keepdims=True),x.shape)
    def allsum(x):
        return jnp.broadcast_to(jnp.sum(x,axis=0,keepdims=True),x.shape)
    NEG=jnp.full((8,tok),-jnp.inf,f32); Z8=jnp.zeros((8,tok),f32)
    def step(i, do1, do2, do3):
        mx=NEG; l8=Z8; D8=Z8
        if do2: m8=stat[0]
        if do3:
            delta8=stat[1]
            dqa=jnp.zeros((HD,tok),f32)
        for c in range(nch):
            if do3:
                e=e_ref[c]
                t=(g8(dp_ref[c])-delta8[None]).astype(bf).reshape(CH,tok)
                g=e*t
                r=jnp.dot(jnp.concatenate([g,e],axis=1),w_ref[...],preferred_element_type=f32)
                acc[c]+=r
                dqa=dqa+jnp.dot(kT[:,c*CH:(c+1)*CH],g,preferred_element_type=f32)
            if do2:
                dp=jnp.dot(kvc(c),dz[i],preferred_element_type=f32)
                e=jnp.exp2((g8(s_ref[c])-m8[None])*c2)
                l8=l8+jnp.sum(e,axis=0)
                D8=D8+jnp.sum(e*g8(dp),axis=0)
                e_ref[c]=e.reshape(CH,tok).astype(bf)
                dp_ref[c]=dp
            if do1:
                s=jnp.dot(kvc(c),qz[i+1],preferred_element_type=f32)
                s_ref[c]=s
                mx=jnp.maximum(mx,jnp.max(g8(s),axis=0))
        if do3:
            dqt[i-1]=(dqa*(stat[2,:1]*scale)).astype(bf)
        if do1: stat[0]=allmax(mx)
        if do2:
            l=allsum(l8); r=1.0/l
            stat[1]=allsum(D8)*r
            stat[2]=r
            wt=jnp.concatenate([(qz[i].astype(f32)*(r[:1]*scale)).astype(bf),(dz[i].astype(f32)*r[:1]).astype(bf)],axis=1)
            w_ref[...]=wt.T
    step(-1,True,False,False)
    step(0,True,True,False)
    def body(i,carry):
        step(i,True,True,True); return carry
    lax.fori_loop(1,heads-1,body,0)
    step(heads-1,False,True,True)
    step(heads,False,False,True)
    dq_ref[...]=dqt[...].reshape(heads*HD,tok).T
    for c in range(nch):
        g_ref[c*CH:(c+1)*CH,:]=acc[c]
def attn_grads(q,d,kvs):
    tok,w=q.shape; heads=w//HD; tiles=len(kvs); nch=tiles*tok//CH
    f32=jnp.float32; bf=jnp.bfloat16
    V=pl.BlockSpec(memory_space=pltpu.VMEM)
    return pl.pallas_call(functools.partial(kernel,heads,tok,tiles),
        out_shape=(jax.ShapeDtypeStruct((tok,w),bf),jax.ShapeDtypeStruct((tiles*tok,2*HD),f32)),
        in_specs=[V]*(2+tiles),out_specs=(V,V),
        scratch_shapes=[pltpu.VMEM((heads,2*HD,tok),bf),pltpu.VMEM((heads,2*HD,tok),bf),pltpu.VMEM((HD,tiles*tok),bf),
          pltpu.VMEM((nch,CH,tok),f32),pltpu.VMEM((nch,CH,tok),f32),pltpu.VMEM((nch,CH,tok),bf),
          pltpu.VMEM((nch,CH,2*HD),f32),pltpu.VMEM((heads,HD,tok),bf),pltpu.VMEM((2*tok,2*HD),bf),pltpu.VMEM((3,8,tok),f32)],
        compiler_params=pltpu.CompilerParams(vmem_limit_bytes=60*2**20),name="attn_grads")(q,d,*kvs)


def shifted(array, axis, by):
    peers = lax.axis_size(axis)
    return lax.ppermute(array, axis, [(i, (i + by) % peers) for i in range(peers)])


STEPS = (("lat", -2), ("lat", 2), ("lon", -2), ("lon", 2))


def local(queries, key_value, dout):
    tile = key_value[0, 0]
    tok = tile.shape[0]
    near = [shifted(tile, axis, by) for axis, by in STEPS]
    dquery, grads = attn_grads(queries[0, 0], dout[0, 0], [tile] + near)
    halves = grads.reshape(5, 2, tok // 2, 2 * HD)
    me = lax.axis_index("head")
    keep = lax.dynamic_index_in_dim(halves, me, 1, keepdims=False)
    send = lax.dynamic_index_in_dim(halves, 1 - me, 1, keepdims=False)
    both = keep + shifted(send, "head", 1)
    total = both[0]
    for index, (axis, by) in enumerate(STEPS):
        back = shifted(both[1 + index].astype(jnp.bfloat16), axis, -by)
        total = total + back.astype(jnp.float32)
    return dquery[None, None], total[None, None]


def solution(mesh):
    placed = (
        P("lat", "lon", None, "head"),
        P("lat", "lon", None, None),
        P("lat", "lon", None, "head"),
    )
    return jax.shard_map(
        local,
        mesh=mesh,
        in_specs=placed,
        out_specs=(P("lat", "lon", None, "head"), P("lat", "lon", "head", None)),
        check_vma=False,
    )
```

```python
import functools

import jax
import jax.numpy as jnp
from jax import lax
from jax.experimental import pallas as pl
from jax.experimental.pallas import tpu as pltpu
from jax.sharding import PartitionSpec as P
HD=64
CH=256
def kernel(heads, tok, tiles, q_ref, d_ref, own_ref, ahead_ref, behind_ref, other_ref,
           dq_ref, gown_ref, gmine_ref, glent_ref,
           qz, dz, kT, s_ref, dp_ref, e_ref, acc, dqt, w_ref, stat):
    kv_refs=[own_ref,ahead_ref,behind_ref,other_ref.at[0],other_ref.at[1]]
    g_refs=[gown_ref,gmine_ref.at[0],gmine_ref.at[1],glent_ref.at[0],glent_ref.at[1]]
    per=tok//CH; nch=tiles*per
    scale=1.0/HD**0.5
    c2=1.4426950408889634*scale
    f32=jnp.float32; bf=jnp.bfloat16
    def kvc(c): return kv_refs[c//per][(c%per)*CH:(c%per+1)*CH,:]
    zero=jnp.zeros((HD,tok),bf)
    qT=q_ref[...].T; dT=d_ref[...].T
    for h in range(heads):
        qz[h,:HD,:]=qT[h*HD:(h+1)*HD,:]; qz[h,HD:,:]=zero
        dz[h,HD:,:]=dT[h*HD:(h+1)*HD,:]; dz[h,:HD,:]=zero
    for c in range(nch):
        kT[:,c*CH:(c+1)*CH]=kvc(c).T[:HD,:]
        acc[c]=jnp.zeros((CH,2*HD),f32)
    def g8(x): return x.reshape(CH//8,8,tok)
    def allmax(x):
        return jnp.broadcast_to(jnp.max(x,axis=0,keepdims=True),x.shape)
    def allsum(x):
        return jnp.broadcast_to(jnp.sum(x,axis=0,keepdims=True),x.shape)
    NEG=jnp.full((8,tok),-jnp.inf,f32); Z8=jnp.zeros((8,tok),f32)
    def step(i, do1, do2, do3):
        mx=NEG; l8=Z8; D8=Z8
        if do2: m8=stat[0]
        if do3:
            delta8=stat[1]
            dqa=jnp.zeros((HD,tok),f32)
        for c in range(nch):
            if do3:
                e=e_ref[c]
                t=(g8(dp_ref[c])-delta8[None]).reshape(CH,tok)
                g=(e.astype(f32)*t).astype(bf)
                r=jnp.dot(jnp.concatenate([g,e],axis=1),w_ref[...],preferred_element_type=f32)
                acc[c]+=r
                dqa=dqa+jnp.dot(kT[:,c*CH:(c+1)*CH],g,preferred_element_type=f32)
            if do2:
                dp=jnp.dot(kvc(c),dz[i],preferred_element_type=f32)
                e=jnp.exp2((g8(s_ref[c])-m8[None])*c2)
                l8=l8+jnp.sum(e,axis=0)
                D8=D8+jnp.sum(e*g8(dp),axis=0)
                e_ref[c]=e.reshape(CH,tok).astype(bf)
                dp_ref[c]=dp
            if do1:
                s=jnp.dot(kvc(c),qz[i+1],preferred_element_type=f32)
                s_ref[c]=s
                mx=jnp.maximum(mx,jnp.max(g8(s),axis=0))
        if do3:
            dqt[i-1]=(dqa*(stat[2,:1]*scale)).astype(bf)
        if do1: stat[0]=allmax(mx)
        if do2:
            l=allsum(l8); r=1.0/l
            stat[1]=allsum(D8)*r
            stat[2]=r
            wt=jnp.concatenate([(qz[i].astype(f32)*(r[:1]*scale)).astype(bf),(dz[i].astype(f32)*r[:1]).astype(bf)],axis=1)
            w_ref[...]=wt.T
    step(-1,True,False,False)
    step(0,True,True,False)
    def body(i,carry):
        step(i,True,True,True); return carry
    lax.fori_loop(1,heads-1,body,0)
    step(heads-1,False,True,True)
    step(heads,False,False,True)
    dq_ref[...]=dqt[...].reshape(heads*HD,tok).T
    for c in range(nch):
        g_refs[c//per][(c%per)*CH:(c%per+1)*CH,:]=acc[c]
def attn_grads(q,d,own,ahead,behind,others):
    tok,w=q.shape; heads=w//HD; tiles=5; nch=tiles*tok//CH
    f32=jnp.float32; bf=jnp.bfloat16
    V=pl.BlockSpec(memory_space=pltpu.VMEM)
    return pl.pallas_call(functools.partial(kernel,heads,tok,tiles),
        out_shape=(jax.ShapeDtypeStruct((tok,w),bf),jax.ShapeDtypeStruct((tok,2*HD),f32),
          jax.ShapeDtypeStruct((2,tok,2*HD),f32),jax.ShapeDtypeStruct((2,tok,2*HD),f32)),
        in_specs=[V]*6,out_specs=(V,V,V,V),
        scratch_shapes=[pltpu.VMEM((heads,2*HD,tok),bf),pltpu.VMEM((heads,2*HD,tok),bf),pltpu.VMEM((HD,tiles*tok),bf),
          pltpu.VMEM((nch,CH,tok),f32),pltpu.VMEM((nch,CH,tok),f32),pltpu.VMEM((nch,CH,tok),bf),
          pltpu.VMEM((nch,CH,2*HD),f32),pltpu.VMEM((heads,HD,tok),bf),pltpu.VMEM((2*tok,2*HD),bf),pltpu.VMEM((3,8,tok),f32)],
        compiler_params=pltpu.CompilerParams(vmem_limit_bytes=60*2**20),name="attn_grads")(q,d,own,ahead,behind,others)


AXES = ("lat", "lon", "head")


def partnered(array):
    return lax.ppermute(array, "head", [(0, 1), (1, 0)])


def spread(array, by):
    nlat, nlon = lax.axis_size("lat"), lax.axis_size("lon")
    pairs = []
    for i in range(nlat):
        for j in range(nlon):
            here = (i * nlon + j) * 2
            pairs.append((here, (((i + by) % nlat) * nlon + j) * 2))
            pairs.append((here + 1, (i * nlon + (j + by) % nlon) * 2 + 1))
    return lax.ppermute(array, AXES, pairs)


def local(queries, key_value, dout):
    bf = jnp.bfloat16
    f32 = jnp.float32
    tile = key_value[0, 0]
    tok = tile.shape[0]
    ahead = spread(tile, -2)
    behind = spread(tile, 2)
    others = partnered(jnp.stack([ahead, behind]))
    dquery, own, mine, lent = attn_grads(
        queries[0, 0], dout[0, 0], tile, ahead, behind, others
    )
    both = mine + partnered(lent)
    back = spread(both[0].astype(bf), 2).astype(f32)
    forth = spread(both[1].astype(bf), -2).astype(f32)
    total = (own + back + forth).reshape(2, tok // 2, 2 * HD)
    me = lax.axis_index("head")
    keep = lax.dynamic_index_in_dim(total, me, 0, keepdims=False)
    send = lax.dynamic_index_in_dim(total, 1 - me, 0, keepdims=False)
    return dquery[None, None], (keep + partnered(send))[None, None]


def solution(mesh):
    placed = (
        P("lat", "lon", None, "head"),
        P("lat", "lon", None, None),
        P("lat", "lon", None, "head"),
    )
    return jax.shard_map(
        local,
        mesh=mesh,
        in_specs=placed,
        out_specs=(P("lat", "lon", None, "head"), P("lat", "lon", "head", None)),
        check_vma=False,
    )
```

```python
import functools

import jax
import jax.numpy as jnp
from jax import lax
from jax.experimental import pallas as pl
from jax.experimental.pallas import tpu as pltpu
from jax.sharding import PartitionSpec as P

HD = 64
CH = 128
TILES = 5
AXES = ("lat", "lon", "head")
SCALE = 1.0 / HD**0.5
LOG2E = 1.4426950408889634
F32 = jnp.float32
BF16 = jnp.bfloat16
VMEM = pl.BlockSpec(memory_space=pltpu.VMEM)


def dot(a, b):
    return jnp.dot(a, b, preferred_element_type=F32)


def prepare_kernel(heads, tok, q_ref, d_ref, qz, dz):
    zero = jnp.zeros((HD, tok), BF16)
    q_t = q_ref[...].T
    d_t = d_ref[...].T
    for h in range(heads):
        qz[h, :HD, :] = q_t[h * HD : (h + 1) * HD, :]
        qz[h, HD:, :] = zero
        dz[h, HD:, :] = d_t[h * HD : (h + 1) * HD, :]
        dz[h, :HD, :] = zero


def main_kernel(
    heads, tok, qz, dz, own_ref, ahead_ref, behind_ref, other0_ref, other1_ref,
    mine_ref, lent_ref, kt_ref, g0, g1, g2, g3, g4, eown_ref, w_ref, r_ref,
    s_ref, dp_ref, e_ref, acc, stat,
):
    kv_refs = [own_ref, ahead_ref, behind_ref, other0_ref, other1_ref]
    g_refs = [g0, g1, g2, g3, g4]
    per = tok // CH
    chunks = TILES * per

    def kv(c):
        return kv_refs[c // per][(c % per) * CH : (c % per + 1) * CH, :]

    def rows8(x):
        return x.reshape(CH // 8, 8, tok)

    def allmax(x):
        return jnp.broadcast_to(jnp.max(x, axis=0, keepdims=True), x.shape)

    def allsum(x):
        return jnp.broadcast_to(jnp.sum(x, axis=0, keepdims=True), x.shape)

    for c in range(chunks):
        kt_ref[:, c * CH : (c + 1) * CH] = kv(c).T[:HD, :]
        if c >= per:
            acc[c - per] = jnp.zeros((CH, 2 * HD), F32)

    def step(i, scores, softmax, grads):
        zeros8 = jnp.zeros((8, tok), F32)
        top, total, delta = jnp.full((8, tok), -jnp.inf, F32), zeros8, zeros8
        if softmax:
            top8 = stat[0]
        if grads:
            delta8 = stat[1]
        for c in range(chunks):
            if grads:
                e = e_ref[c]
                t = (rows8(dp_ref[c]) - delta8[None]).reshape(CH, tok)
                g = (e.astype(F32) * t).astype(BF16)
                g_refs[c // per][i - 1, c % per] = g
                if c < per:
                    eown_ref[i - 1, c] = e
                else:
                    acc[c - per] += dot(jnp.concatenate([g, e], axis=1), w_ref[i - 1])
            if softmax:
                dp = dot(kv(c), dz[i])
                e = jnp.exp2((rows8(s_ref[c]) - top8[None]) * (LOG2E * SCALE))
                total = total + jnp.sum(e, axis=0)
                delta = delta + jnp.sum(e * rows8(dp), axis=0)
                e_ref[c] = e.reshape(CH, tok).astype(BF16)
                dp_ref[c] = dp
            if scores:
                s = dot(kv(c), qz[i + 1])
                s_ref[c] = s
                top = jnp.maximum(top, jnp.max(rows8(s), axis=0))
        if scores:
            stat[0] = allmax(top)
        if softmax:
            r = 1.0 / allsum(total)
            stat[1] = allsum(delta) * r
            r_ref[i] = r * SCALE
            wq = (qz[i].astype(F32) * (r[:1] * SCALE)).astype(BF16)
            wd = (dz[i].astype(F32) * r[:1]).astype(BF16)
            w_ref[i] = jnp.concatenate([wq, wd], axis=1).T

    step(-1, True, False, False)
    step(0, True, True, False)

    def body(i, carry):
        step(i, True, True, True)
        return carry

    lax.fori_loop(1, heads - 1, body, 0)
    step(heads - 1, False, True, True)
    step(heads, False, False, True)
    for c in range(per, chunks):
        rows = slice((c % per) * CH, (c % per + 1) * CH)
        if c < 3 * per:
            mine_ref[c // per - 1, rows, :] = acc[c - per]
        else:
            lent_ref[c // per - 3, rows, :] = acc[c - per].astype(BF16)


def combine_kernel(mine_ref, theirs_ref, back_ref, forth_ref):
    back_ref[...] = (mine_ref[0] + theirs_ref[0].astype(F32)).astype(BF16)
    forth_ref[...] = (mine_ref[1] + theirs_ref[1].astype(F32)).astype(BF16)


def finish_kernel(
    heads, tok, kt_ref, g0, g1, g2, g3, g4, eown_ref, w_ref, r_ref, after_ref,
    dq_ref, own_ref, dqt, acc,
):
    per = tok // CH

    def body(h, carry):
        g = jnp.concatenate([x[h].reshape(tok, tok) for x in (g0, g1, g2, g3, g4)], axis=0)
        dqt[h] = (dot(kt_ref[...], g) * r_ref[h, :1]).astype(BF16)
        ge = jnp.concatenate([g[:tok], eown_ref[h].reshape(tok, tok)], axis=1)
        acc[...] += dot(ge, w_ref[h])
        return carry

    acc[...] = jnp.zeros_like(acc)
    lax.fori_loop(0, heads, body, 0)
    dq_ref[...] = dqt[...].reshape(heads * HD, tok).T
    own_ref[...] = acc[...]


def settle_kernel(half, own_ref, back_ref, forth_ref, keep_ref, send_ref):
    me = lax.axis_index("head")

    def half_of(which):
        rows = pl.ds(pl.multiple_of(which * half, half), half)
        back = back_ref[rows, :].astype(F32)
        return own_ref[rows, :] + back + forth_ref[rows, :].astype(F32)

    keep_ref[...] = half_of(me)
    send_ref[...] = half_of(1 - me)


def shape(dims, dtype):
    return jax.ShapeDtypeStruct(dims, dtype)


def call(kernel, name, outs, scratch, mib, flops, operands, flags=None):
    return pl.pallas_call(
        kernel,
        name=name,
        out_shape=outs,
        in_specs=[VMEM] * len(operands),
        out_specs=tuple([VMEM] * len(outs)),
        scratch_shapes=scratch,
        cost_estimate=pl.CostEstimate(flops=flops, bytes_accessed=2**20, transcendentals=0),
        compiler_params=pltpu.CompilerParams(vmem_limit_bytes=mib * 2**20, flags=flags),
    )(*operands)


def partnered(array):
    return lax.ppermute(array, "head", [(0, 1), (1, 0)])


def spread(array, by):
    nlat, nlon = lax.axis_size("lat"), lax.axis_size("lon")
    pairs = []
    for i in range(nlat):
        for j in range(nlon):
            here = (i * nlon + j) * 2
            pairs.append((here, (((i + by) % nlat) * nlon + j) * 2))
            pairs.append((here + 1, (i * nlon + (j + by) % nlon) * 2 + 1))
    return lax.ppermute(array, AXES, pairs)


def local(queries, key_value, dout):
    tile = key_value[0, 0]
    tok, width = queries.shape[2:]
    heads = width // HD
    chunks = TILES * tok // CH
    ahead = spread(tile, -2)
    behind = spread(tile, 2)
    qz, dz = call(
        functools.partial(prepare_kernel, heads, tok), "prepare",
        (shape((heads, 2 * HD, tok), BF16),) * 2, [], 8, 10**9,
        (queries[0, 0], dout[0, 0]),
    )
    ahead, behind, qz, dz = lax.optimization_barrier((ahead, behind, qz, dz))
    other0, other1 = partnered(ahead), partnered(behind)
    mine, lent, kt, *g, eown, w, r = call(
        functools.partial(main_kernel, heads, tok), "main",
        (
            shape((2, tok, 2 * HD), F32), shape((2, tok, 2 * HD), BF16),
            shape((HD, TILES * tok), BF16),
            *[shape((heads, tok // CH, CH, tok), BF16)] * (TILES + 1),
            shape((heads, 2 * tok, 2 * HD), BF16), shape((heads, 8, tok), F32),
        ),
        [
            pltpu.VMEM((chunks, CH, tok), F32), pltpu.VMEM((chunks, CH, tok), F32),
            pltpu.VMEM((chunks, CH, tok), BF16),
            pltpu.VMEM((chunks - tok // CH, CH, 2 * HD), F32), pltpu.VMEM((2, 8, tok), F32),
        ],
        24, 10**10, (qz, dz, tile, ahead, behind, other0, other1),
    )
    low0, low1 = call(
        combine_kernel, "combine", (shape((tok, 2 * HD), BF16),) * 2, [], 4, 10**6,
        (mine, partnered(lent)),
    )
    back, forth = spread(low0, 2), spread(low1, -2)
    dquery, own = call(
        functools.partial(finish_kernel, heads, tok), "finish",
        (shape((tok, width), BF16), shape((tok, 2 * HD), F32)),
        [pltpu.VMEM((heads, HD, tok), BF16), pltpu.VMEM((tok, 2 * HD), F32)],
        8, 3 * 10**9, (kt, *g, eown, w, r, low0),
    )
    keep, send = call(
        functools.partial(settle_kernel, tok // 2), "settle",
        (shape((tok // 2, 2 * HD), F32),) * 2, [], 4, 10**6, (own, back, forth),
    )
    return dquery[None, None], (keep + partnered(send))[None, None]


def solution(mesh):
    placed = (
        P("lat", "lon", None, "head"),
        P("lat", "lon", None, None),
        P("lat", "lon", None, "head"),
    )
    return jax.shard_map(
        local,
        mesh=mesh,
        in_specs=placed,
        out_specs=(P("lat", "lon", None, "head"), P("lat", "lon", "head", None)),
        check_vma=False,
    )
```

```python
import functools

import jax
import jax.numpy as jnp
from jax import lax
from jax.experimental import pallas as pl
from jax.experimental.pallas import tpu as pltpu
from jax.sharding import PartitionSpec as P

HD = 64
CH = 256
TILES = 5
AXES = ("lat", "lon", "head")
SCALE = 1.0 / HD**0.5
LOG2E = 1.4426950408889634
F32 = jnp.float32
BF16 = jnp.bfloat16
VMEM = pl.BlockSpec(memory_space=pltpu.VMEM)


def dot(a, b):
    return jnp.dot(a, b, preferred_element_type=F32)


def prepare_kernel(heads, tok, q_ref, d_ref, tile_ref, qz, dz, own_ref):
    own_ref[...] = tile_ref[...]
    zero = jnp.zeros((HD, tok), BF16)
    q_t = q_ref[...].T
    d_t = d_ref[...].T
    for h in range(heads):
        qz[h, :HD, :] = q_t[h * HD : (h + 1) * HD, :]
        qz[h, HD:, :] = zero
        dz[h, HD:, :] = d_t[h * HD : (h + 1) * HD, :]
        dz[h, :HD, :] = zero


def main_kernel(
    heads, tok, qz, dz, own_ref, ahead_ref, behind_ref, other0_ref, other1_ref,
    mine_ref, lent_ref, kt_ref, g0, g1, g2, g3, g4, eown_ref, w_ref, r_ref,
    s_ref, dp_ref, e_ref, acc, stat,
):
    kv_refs = [own_ref, ahead_ref, behind_ref, other0_ref, other1_ref]
    g_refs = [g0, g1, g2, g3, g4]
    per = tok // CH
    chunks = TILES * per

    def kv(c):
        return kv_refs[c // per][(c % per) * CH : (c % per + 1) * CH, :]

    def rows8(x):
        return x.reshape(CH // 8, 8, tok)

    def allmax(x):
        return jnp.broadcast_to(jnp.max(x, axis=0, keepdims=True), x.shape)

    def allsum(x):
        return jnp.broadcast_to(jnp.sum(x, axis=0, keepdims=True), x.shape)

    def step(i, scores, softmax, grads):
        zeros8 = jnp.zeros((8, tok), F32)
        top, total, delta = jnp.full((8, tok), -jnp.inf, F32), zeros8, zeros8
        if softmax:
            top8 = stat[0]
        if grads:
            delta8 = stat[1]
            held = []
        for c in range(chunks):
            if grads:
                e = e_ref[c]
                t = (rows8(dp_ref[c]) - delta8[None]).astype(BF16).reshape(CH, tok)
                g = e * t
                g_refs[c // per][i - 1, c % per] = g
                if c < per:
                    eown_ref[i - 1, c] = e
                else:
                    held.append((g, e))
                if len(held) == 1:
                    gt, et = (jnp.concatenate(x, axis=0).T for x in zip(*held))
                    pair = c - per
                    acc[pair, :HD] += dot(w_ref[i - 1, :HD], gt)
                    acc[pair, HD:] += dot(w_ref[i - 1, HD:], et)
                    held = []
            if softmax:
                dp = dot(kv(c), dz[i])
                e = jnp.exp2((rows8(s_ref[c]) - top8[None]) * (LOG2E * SCALE))
                total = total + jnp.sum(e, axis=0)
                delta = delta + jnp.sum(e * rows8(dp), axis=0)
                e_ref[c] = e.reshape(CH, tok).astype(BF16)
                dp_ref[c] = dp
                if not grads and c >= per:
                    acc[c - per] = jnp.zeros((2 * HD, CH), F32)
            if scores:
                s = dot(kv(c), qz[i + 1])
                s_ref[c] = s
                if not softmax:
                    kt_ref[:, c * CH : (c + 1) * CH] = kv(c).T[:HD, :]
                top = jnp.maximum(top, jnp.max(rows8(s), axis=0))
        if scores:
            stat[0] = allmax(top)
        if softmax:
            r = 1.0 / allsum(total)
            stat[1] = allsum(delta) * r
            r_ref[i] = r * SCALE
            w_ref[i, :HD] = (qz[i, :HD].astype(F32) * (r[:1] * SCALE)).astype(BF16)
            w_ref[i, HD:] = (dz[i, HD:].astype(F32) * r[:1]).astype(BF16)

    step(-1, True, False, False)
    step(0, True, True, False)

    def body(i, carry):
        step(i, True, True, True)
        return carry

    lax.fori_loop(1, heads - 1, body, 0)
    step(heads - 1, False, True, True)
    step(heads, False, False, True)
    for c in range(0, chunks - per):
        rows = slice((c % per) * CH, (c % per + 1) * CH)
        grad = acc[c].T
        if c < 2 * per:
            mine_ref[c // per, rows, :] = grad
        else:
            lent_ref[c // per - 2, rows, :] = grad.astype(BF16)


def combine_kernel(mine_ref, theirs_ref, back_ref, forth_ref):
    back_ref[...] = (mine_ref[0] + theirs_ref[0].astype(F32)).astype(BF16)
    forth_ref[...] = (mine_ref[1] + theirs_ref[1].astype(F32)).astype(BF16)


def finish_kernel(
    heads, tok, kt_ref, g0, g1, g2, g3, g4, eown_ref, w_ref, r_ref, after_ref,
    dq_ref, own_ref, dqt, acc,
):
    per = tok // CH

    def body(h, carry):
        g = jnp.concatenate([x[h].reshape(tok, tok) for x in (g0, g1, g2, g3, g4)], axis=0)
        dqt[h] = (dot(kt_ref[...], g) * r_ref[h, :1]).astype(BF16)
        acc[:HD] += dot(w_ref[h, :HD], g[:tok].T)
        acc[HD:] += dot(w_ref[h, HD:], eown_ref[h].reshape(tok, tok).T)
        return carry

    acc[...] = jnp.zeros_like(acc)
    lax.fori_loop(0, heads, body, 0, unroll=4)
    dq_ref[...] = dqt[...].reshape(heads * HD, tok).T
    own_ref[...] = acc[...].T


def settle_kernel(half, own_ref, back_ref, forth_ref, keep_ref, send_ref):
    me = lax.axis_index("head")

    def half_of(which):
        rows = pl.ds(pl.multiple_of(which * half, half), half)
        back = back_ref[rows, :].astype(F32)
        return own_ref[rows, :] + back + forth_ref[rows, :].astype(F32)

    keep_ref[...] = half_of(me)
    send_ref[...] = half_of(1 - me)


def shape(dims, dtype):
    return jax.ShapeDtypeStruct(dims, dtype)


def call(kernel, name, outs, scratch, mib, flops, operands, flags=None):
    return pl.pallas_call(
        kernel,
        name=name,
        out_shape=outs,
        in_specs=[VMEM] * len(operands),
        out_specs=tuple([VMEM] * len(outs)),
        scratch_shapes=scratch,
        cost_estimate=pl.CostEstimate(flops=flops, bytes_accessed=2**20, transcendentals=0),
        compiler_params=pltpu.CompilerParams(vmem_limit_bytes=mib * 2**20, flags=flags),
    )(*operands)


def partnered(array):
    return lax.ppermute(array, "head", [(0, 1), (1, 0)])


def spread(array, by, turned):
    nlat, nlon = lax.axis_size("lat"), lax.axis_size("lon")
    pairs = []
    for i in range(nlat):
        for j in range(nlon):
            here = (i * nlon + j) * 2
            along_lat = (((i + by) % nlat) * nlon + j) * 2
            along_lon = (i * nlon + (j + by) % nlon) * 2
            pairs.append((here + turned, along_lat + turned))
            pairs.append((here + 1 - turned, along_lon + 1 - turned))
    return lax.ppermute(array, AXES, pairs)


def local(queries, key_value, dout):
    tile = key_value[0, 0]
    tok, width = queries.shape[2:]
    heads = width // HD
    chunks = TILES * tok // CH
    ahead = spread(tile, -2, 0)
    behind = spread(tile, 2, 1)
    qz, dz, mid = call(
        functools.partial(prepare_kernel, heads, tok), "prepare",
        (*[shape((heads, 2 * HD, tok), BF16)] * 2, shape((tok, 2 * HD), BF16)), [], 8, 10**9,
        (queries[0, 0], dout[0, 0], tile),
    )
    ahead, behind, qz, dz = lax.optimization_barrier((ahead, behind, qz, dz))
    other0, other1 = partnered(ahead), partnered(behind)
    mine, lent, kt, *g, eown, w, r = call(
        functools.partial(main_kernel, heads, tok), "main",
        (
            shape((2, tok, 2 * HD), F32), shape((2, tok, 2 * HD), BF16),
            shape((HD, TILES * tok), BF16),
            *[shape((heads, tok // CH, CH, tok), BF16)] * (TILES + 1),
            shape((heads, 2 * HD, tok), BF16), shape((heads, 8, tok), F32),
        ),
        [
            pltpu.VMEM((chunks, CH, tok), F32), pltpu.VMEM((chunks, CH, tok), F32),
            pltpu.VMEM((chunks, CH, tok), BF16),
            pltpu.VMEM((chunks - tok // CH, 2 * HD, CH), F32), pltpu.VMEM((2, 8, tok), F32),
        ],
        24, 10**10, (qz, dz, mid, ahead, behind, other0, other1),
    )
    low0, low1 = call(
        combine_kernel, "combine", (shape((tok, 2 * HD), BF16),) * 2, [], 4, 10**6,
        (mine, partnered(lent)),
    )
    back, forth = spread(low0, 2, 0), spread(low1, -2, 1)
    dquery, own = call(
        functools.partial(finish_kernel, heads, tok), "finish",
        (shape((tok, width), BF16), shape((tok, 2 * HD), F32)),
        [pltpu.VMEM((heads, HD, tok), BF16), pltpu.VMEM((2 * HD, tok), F32)],
        8, 3 * 10**9, (kt, *g, eown, w, r, low0),
    )
    keep, send = call(
        functools.partial(settle_kernel, tok // 2), "settle",
        (shape((tok // 2, 2 * HD), F32),) * 2, [], 4, 10**6, (own, back, forth),
    )
    return dquery[None, None], (keep + partnered(send))[None, None]


def solution(mesh):
    placed = (
        P("lat", "lon", None, "head"),
        P("lat", "lon", None, None),
        P("lat", "lon", None, "head"),
    )
    return jax.shard_map(
        local,
        mesh=mesh,
        in_specs=placed,
        out_specs=(P("lat", "lon", None, "head"), P("lat", "lon", "head", None)),
        check_vma=False,
    )
```

```python
import functools

import jax
import jax.numpy as jnp
from jax import lax
from jax.experimental import pallas as pl
from jax.experimental.pallas import tpu as pltpu
from jax.sharding import PartitionSpec as P

HD = 64
CH = 256
TILES = 5
AXES = ("lat", "lon", "head")
SCALE = 1.0 / HD**0.5
LOG2E = 1.4426950408889634
F32 = jnp.float32
BF16 = jnp.bfloat16
VMEM = pl.BlockSpec(memory_space=pltpu.VMEM)


def dot(a, b):
    return jnp.dot(a, b, preferred_element_type=F32)


def prepare_kernel(heads, tok, q_ref, d_ref, tile_ref, qz, dz, own_ref):
    own_ref[...] = tile_ref[...]
    zero = jnp.zeros((HD, tok), BF16)
    q_t = q_ref[...].T
    d_t = d_ref[...].T
    for h in range(heads):
        qz[h, :HD, :] = q_t[h * HD : (h + 1) * HD, :]
        qz[h, HD:, :] = zero
        dz[h, HD:, :] = d_t[h * HD : (h + 1) * HD, :]
        dz[h, :HD, :] = zero


def main_kernel(
    heads, tok, qz, dz, own_ref, ahead_ref, behind_ref, other0_ref, other1_ref,
    mine_ref, lent_ref, kt_ref, g0, g1, g2, g3, g4, eown_ref, w_ref, r_ref,
    s_ref, dp_ref, e_ref, acc, stat,
):
    kv_refs = [own_ref, ahead_ref, behind_ref, other0_ref, other1_ref]
    g_refs = [g0, g1, g2, g3, g4]
    per = tok // CH
    chunks = TILES * per

    def kv(c):
        return kv_refs[c // per][(c % per) * CH : (c % per + 1) * CH, :]

    def rows8(x):
        return x.reshape(CH // 8, 8, tok)

    def allmax(x):
        return jnp.broadcast_to(jnp.max(x, axis=0, keepdims=True), x.shape)

    def allsum(x):
        return jnp.broadcast_to(jnp.sum(x, axis=0, keepdims=True), x.shape)

    def step(i, scores, softmax, grads):
        zeros8 = jnp.zeros((8, tok), F32)
        top, total, delta = jnp.full((8, tok), -jnp.inf, F32), zeros8, zeros8
        if softmax:
            top8 = stat[0]
        if grads:
            delta8 = stat[1]
            held = []
        for c in range(chunks):
            if grads:
                e = e_ref[c]
                t = (rows8(dp_ref[c]) - delta8[None]).astype(BF16).reshape(CH, tok)
                g = e * t
                g_refs[c // per][i - 1, c % per] = g
                if c < per:
                    eown_ref[i - 1, c] = e
                else:
                    held.append((g, e))
                if len(held) == 1:
                    gt, et = (jnp.concatenate(x, axis=0).T for x in zip(*held))
                    pair = c - per
                    acc[pair, :HD] += dot(w_ref[i - 1, :HD], gt)
                    acc[pair, HD:] += dot(w_ref[i - 1, HD:], et)
                    held = []
            if softmax:
                dp = dot(kv(c), dz[i])
                e = jnp.exp2((rows8(s_ref[c]) - top8[None]) * (LOG2E * SCALE))
                total = total + jnp.sum(e, axis=0)
                delta = delta + jnp.sum(e * rows8(dp), axis=0)
                e_ref[c] = e.reshape(CH, tok).astype(BF16)
                dp_ref[c] = dp
                if not grads and c >= per:
                    acc[c - per] = jnp.zeros((2 * HD, CH), F32)
            if scores:
                s = dot(kv(c), qz[i + 1])
                s_ref[c] = s
                if not softmax:
                    kt_ref[:, c * CH : (c + 1) * CH] = kv(c).T[:HD, :]
                top = jnp.maximum(top, jnp.max(rows8(s), axis=0))
        if scores:
            stat[0] = allmax(top)
        if softmax:
            r = 1.0 / allsum(total)
            stat[1] = allsum(delta) * r
            r_ref[i] = r * SCALE
            w_ref[i, :HD] = (qz[i, :HD].astype(F32) * (r[:1] * SCALE)).astype(BF16)
            w_ref[i, HD:] = (dz[i, HD:].astype(F32) * r[:1]).astype(BF16)

    step(-1, True, False, False)
    step(0, True, True, False)

    def body(i, carry):
        step(i, True, True, True)
        return carry

    lax.fori_loop(1, heads - 1, body, 0)
    step(heads - 1, False, True, True)
    step(heads, False, False, True)
    for c in range(0, chunks - per):
        rows = slice((c % per) * CH, (c % per + 1) * CH)
        grad = acc[c].T
        if c < 2 * per:
            mine_ref[c // per, rows, :] = grad
        else:
            lent_ref[c // per - 2, rows, :] = grad.astype(BF16)


def combine_kernel(mine_ref, theirs_ref, back_ref, forth_ref):
    back_ref[...] = (mine_ref[0] + theirs_ref[0].astype(F32)).astype(BF16)
    forth_ref[...] = (mine_ref[1] + theirs_ref[1].astype(F32)).astype(BF16)


def finish_kernel(
    heads, tok, kt_ref, g0, g1, g2, g3, g4, eown_ref, w_ref, r_ref, after_ref,
    dq_ref, own_ref, dqt, acc,
):
    per = tok // CH

    def body(h, carry):
        g = jnp.concatenate([x[h].reshape(tok, tok) for x in (g0, g1, g2, g3, g4)], axis=0)
        dqt[h] = (dot(kt_ref[...], g) * r_ref[h, :1]).astype(BF16)
        acc[:HD] += dot(w_ref[h, :HD], g[:tok].T)
        acc[HD:] += dot(w_ref[h, HD:], eown_ref[h].reshape(tok, tok).T)
        return carry

    acc[...] = jnp.zeros_like(acc)
    lax.fori_loop(0, heads, body, 0, unroll=4)
    dq_ref[...] = dqt[...].reshape(heads * HD, tok).T
    own_ref[...] = acc[...].T


def settle_kernel(half, own_ref, back_ref, forth_ref, keep_ref, send_ref):
    me = lax.axis_index("head")

    def half_of(which):
        rows = pl.ds(pl.multiple_of(which * half, half), half)
        back = back_ref[rows, :].astype(F32)
        return own_ref[rows, :] + back + forth_ref[rows, :].astype(F32)

    keep_ref[...] = half_of(me)
    send_ref[...] = half_of(1 - me)


def shape(dims, dtype):
    return jax.ShapeDtypeStruct(dims, dtype)


def call(kernel, name, outs, scratch, mib, flops, operands, flags=None):
    return pl.pallas_call(
        kernel,
        name=name,
        out_shape=outs,
        in_specs=[VMEM] * len(operands),
        out_specs=tuple([VMEM] * len(outs)),
        scratch_shapes=scratch,
        cost_estimate=pl.CostEstimate(flops=flops, bytes_accessed=2**20, transcendentals=0),
        compiler_params=pltpu.CompilerParams(vmem_limit_bytes=mib * 2**20, flags=flags),
    )(*operands)


def partnered(array):
    return lax.ppermute(array, "head", [(0, 1), (1, 0)])


def mate(k, size, odd):
    place = k // 2
    place = place + 1 if (place + odd) % 2 == 0 else place - 1
    return place % (size // 2) * 2 + k % 2


def swap(array, odd):
    nlat, nlon = lax.axis_size("lat"), lax.axis_size("lon")
    pairs = []
    for i in range(nlat):
        for j in range(nlon):
            here = (i * nlon + j) * 2
            along_lat = (mate(i, nlat, odd) * nlon + j) * 2
            along_lon = (i * nlon + mate(j, nlon, odd)) * 2
            core = 0
            pairs.append((here + core, along_lat + core))
            pairs.append((here + 1 - core, along_lon + 1 - core))
    return lax.ppermute(array, AXES, pairs)


def local(queries, key_value, dout):
    tile = key_value[0, 0]
    tok, width = queries.shape[2:]
    heads = width // HD
    chunks = TILES * tok // CH
    ahead = swap(tile, 0)
    behind = swap(tile, 1)
    qz, dz, mid = call(
        functools.partial(prepare_kernel, heads, tok), "prepare",
        (*[shape((heads, 2 * HD, tok), BF16)] * 2, shape((tok, 2 * HD), BF16)), [], 8, 10**9,
        (queries[0, 0], dout[0, 0], tile),
    )
    ahead, behind, qz, dz = lax.optimization_barrier((ahead, behind, qz, dz))
    other0, other1 = partnered(ahead), partnered(behind)
    mine, lent, kt, *g, eown, w, r = call(
        functools.partial(main_kernel, heads, tok), "main",
        (
            shape((2, tok, 2 * HD), F32), shape((2, tok, 2 * HD), BF16),
            shape((HD, TILES * tok), BF16),
            *[shape((heads, tok // CH, CH, tok), BF16)] * (TILES + 1),
            shape((heads, 2 * HD, tok), BF16), shape((heads, 8, tok), F32),
        ),
        [
            pltpu.VMEM((chunks, CH, tok), F32), pltpu.VMEM((chunks, CH, tok), F32),
            pltpu.VMEM((chunks, CH, tok), BF16),
            pltpu.VMEM((chunks - tok // CH, 2 * HD, CH), F32), pltpu.VMEM((2, 8, tok), F32),
        ],
        24, 10**10, (qz, dz, mid, ahead, behind, other0, other1),
    )
    low0, low1 = call(
        combine_kernel, "combine", (shape((tok, 2 * HD), BF16),) * 2, [], 4, 10**6,
        (mine, partnered(lent)),
    )
    back, forth = swap(low0, 0), swap(low1, 1)
    dquery, own = call(
        functools.partial(finish_kernel, heads, tok), "finish",
        (shape((tok, width), BF16), shape((tok, 2 * HD), F32)),
        [pltpu.VMEM((heads, HD, tok), BF16), pltpu.VMEM((2 * HD, tok), F32)],
        8, 3 * 10**9, (kt, *g, eown, w, r, low0),
    )
    keep, send = call(
        functools.partial(settle_kernel, tok // 2), "settle",
        (shape((tok // 2, 2 * HD), F32),) * 2, [], 4, 10**6, (own, back, forth),
    )
    return dquery[None, None], (keep + partnered(send))[None, None]


def solution(mesh):
    placed = (
        P("lat", "lon", None, "head"),
        P("lat", "lon", None, None),
        P("lat", "lon", None, "head"),
    )
    return jax.shard_map(
        local,
        mesh=mesh,
        in_specs=placed,
        out_specs=(P("lat", "lon", None, "head"), P("lat", "lon", "head", None)),
        check_vma=False,
    )
```

```python
import functools

import jax
import jax.numpy as jnp
from jax import lax
from jax.experimental import pallas as pl
from jax.experimental.pallas import tpu as pltpu
from jax.sharding import PartitionSpec as P

HD = 64
CH = 256
TILES = 5
AXES = ("lat", "lon", "head")
SCALE = 1.0 / HD**0.5
LOG2E = 1.4426950408889634
F32 = jnp.float32
BF16 = jnp.bfloat16
VMEM = pl.BlockSpec(memory_space=pltpu.VMEM)


def dot(a, b):
    return jnp.dot(a, b, preferred_element_type=F32)


def prepare_kernel(heads, tok, q_ref, d_ref, tile_ref, qz, dz, own_ref):
    own_ref[...] = tile_ref[...]
    zero = jnp.zeros((HD, tok), BF16)
    q_t = q_ref[...].T
    d_t = d_ref[...].T
    for h in range(heads):
        qz[h, :HD, :] = q_t[h * HD : (h + 1) * HD, :]
        qz[h, HD:, :] = zero
        dz[h, HD:, :] = d_t[h * HD : (h + 1) * HD, :]
        dz[h, :HD, :] = zero


def main_kernel(
    heads, tok, qz, dz, own_ref, ahead_ref, behind_ref, other0_ref, other1_ref,
    mine_ref, lent_ref, kt_ref, g0, g1, g2, g3, g4, eown_ref, w_ref, r_ref,
    s_ref, dp_ref, e_ref, acc, stat,
):
    kv_refs = [own_ref, ahead_ref, behind_ref, other0_ref, other1_ref]
    g_refs = [g0, g1, g2, g3, g4]
    per = tok // CH
    chunks = TILES * per

    def kv(c):
        return kv_refs[c // per][(c % per) * CH : (c % per + 1) * CH, :]

    def rows8(x):
        return x.reshape(CH // 8, 8, tok)

    def allmax(x):
        return jnp.broadcast_to(jnp.max(x, axis=0, keepdims=True), x.shape)

    def allsum(x):
        return jnp.broadcast_to(jnp.sum(x, axis=0, keepdims=True), x.shape)

    def step(i, scores, softmax, grads):
        zeros8 = jnp.zeros((8, tok), F32)
        top, total, delta = jnp.full((8, tok), -jnp.inf, F32), zeros8, zeros8
        if softmax:
            top8 = stat[0]
        if grads:
            delta8 = stat[1]
            held = []
        for c in range(chunks):
            if grads:
                e = e_ref[c]
                t = (rows8(dp_ref[c]) - delta8[None]).astype(BF16).reshape(CH, tok)
                g = e * t
                g_refs[c // per][i - 1, c % per] = g
                if c < per:
                    eown_ref[i - 1, c] = e
                else:
                    held.append((g, e))
                if len(held) == 1:
                    gt, et = (jnp.concatenate(x, axis=0).T for x in zip(*held))
                    pair = c - per
                    acc[pair, :HD] += dot(w_ref[i - 1, :HD], gt)
                    acc[pair, HD:] += dot(w_ref[i - 1, HD:], et)
                    held = []
            if softmax:
                dp = dot(kv(c), dz[i])
                e = jnp.exp2((rows8(s_ref[c]) - top8[None]) * (LOG2E * SCALE))
                total = total + jnp.sum(e, axis=0)
                delta = delta + jnp.sum(e * rows8(dp), axis=0)
                e_ref[c] = e.reshape(CH, tok).astype(BF16)
                dp_ref[c] = dp
                if not grads and c >= per:
                    acc[c - per] = jnp.zeros((2 * HD, CH), F32)
            if scores:
                s = dot(kv(c), qz[i + 1])
                s_ref[c] = s
                if not softmax:
                    kt_ref[:, c * CH : (c + 1) * CH] = kv(c).T[:HD, :]
                top = jnp.maximum(top, jnp.max(rows8(s), axis=0))
        if scores:
            stat[0] = allmax(top)
        if softmax:
            r = 1.0 / allsum(total)
            stat[1] = allsum(delta) * r
            r_ref[i] = r * SCALE
            w_ref[i, :HD] = (qz[i, :HD].astype(F32) * (r[:1] * SCALE)).astype(BF16)
            w_ref[i, HD:] = (dz[i, HD:].astype(F32) * r[:1]).astype(BF16)

    step(-1, True, False, False)
    step(0, True, True, False)

    def body(i, carry):
        step(i, True, True, True)
        return carry

    lax.fori_loop(1, heads - 1, body, 0)
    step(heads - 1, False, True, True)
    step(heads, False, False, True)
    for c in range(0, chunks - per):
        rows = slice((c % per) * CH, (c % per + 1) * CH)
        grad = acc[c].T
        if c < 2 * per:
            mine_ref[c // per, rows, :] = grad
        else:
            lent_ref[c // per - 2, rows, :] = grad.astype(BF16)


def combine_kernel(mine_ref, theirs_ref, back_ref, forth_ref):
    back_ref[...] = (mine_ref[0] + theirs_ref[0].astype(F32)).astype(BF16)
    forth_ref[...] = (mine_ref[1] + theirs_ref[1].astype(F32)).astype(BF16)


def finish_kernel(
    heads, tok, kt_ref, g0, g1, g2, g3, g4, eown_ref, w_ref, r_ref, after_ref,
    dqt, own_ref, acc,
):
    per = tok // CH

    def body(h, carry):
        g = jnp.concatenate([x[h].reshape(tok, tok) for x in (g0, g1, g2, g3, g4)], axis=0)
        dqt[h] = (dot(kt_ref[...], g) * r_ref[h, :1]).astype(BF16)
        acc[:HD] += dot(w_ref[h, :HD], g[:tok].T)
        acc[HD:] += dot(w_ref[h, HD:], eown_ref[h].reshape(tok, tok).T)
        return carry

    acc[...] = jnp.zeros_like(acc)
    lax.fori_loop(0, heads, body, 0, unroll=4)
    own_ref[...] = acc[...].T


def tail_kernel(heads, tok, dqt, after_ref, dq_ref):
    dq_ref[...] = dqt[...].reshape(heads * HD, tok).T


def settle_kernel(half, own_ref, back_ref, forth_ref, keep_ref, send_ref):
    me = lax.axis_index("head")

    def half_of(which):
        rows = pl.ds(pl.multiple_of(which * half, half), half)
        back = back_ref[rows, :].astype(F32)
        return own_ref[rows, :] + back + forth_ref[rows, :].astype(F32)

    keep_ref[...] = half_of(me)
    send_ref[...] = half_of(1 - me)


def shape(dims, dtype):
    return jax.ShapeDtypeStruct(dims, dtype)


def call(kernel, name, outs, scratch, mib, flops, operands, flags=None):
    return pl.pallas_call(
        kernel,
        name=name,
        out_shape=outs,
        in_specs=[VMEM] * len(operands),
        out_specs=tuple([VMEM] * len(outs)),
        scratch_shapes=scratch,
        cost_estimate=pl.CostEstimate(flops=flops, bytes_accessed=2**20, transcendentals=0),
        compiler_params=pltpu.CompilerParams(vmem_limit_bytes=mib * 2**20, flags=flags),
    )(*operands)


def partnered(array):
    return lax.ppermute(array, "head", [(0, 1), (1, 0)])


def mate(k, size, odd):
    place = k // 2
    place = place + 1 if (place + odd) % 2 == 0 else place - 1
    return place % (size // 2) * 2 + k % 2


def swap(array, odd):
    nlat, nlon = lax.axis_size("lat"), lax.axis_size("lon")
    pairs = []
    for i in range(nlat):
        for j in range(nlon):
            here = (i * nlon + j) * 2
            along_lat = (mate(i, nlat, odd) * nlon + j) * 2
            along_lon = (i * nlon + mate(j, nlon, odd)) * 2
            core = 0
            pairs.append((here + core, along_lat + core))
            pairs.append((here + 1 - core, along_lon + 1 - core))
    return lax.ppermute(array, AXES, pairs)


def local(queries, key_value, dout):
    tile = key_value[0, 0]
    tok, width = queries.shape[2:]
    heads = width // HD
    chunks = TILES * tok // CH
    ahead = swap(tile, 0)
    behind = swap(tile, 1)
    qz, dz, mid = call(
        functools.partial(prepare_kernel, heads, tok), "prepare",
        (*[shape((heads, 2 * HD, tok), BF16)] * 2, shape((tok, 2 * HD), BF16)), [], 8, 10**9,
        (queries[0, 0], dout[0, 0], tile),
    )
    ahead, behind, qz, dz = lax.optimization_barrier((ahead, behind, qz, dz))
    other0, other1 = partnered(ahead), partnered(behind)
    mine, lent, kt, *g, eown, w, r = call(
        functools.partial(main_kernel, heads, tok), "main",
        (
            shape((2, tok, 2 * HD), F32), shape((2, tok, 2 * HD), BF16),
            shape((HD, TILES * tok), BF16),
            *[shape((heads, tok // CH, CH, tok), BF16)] * (TILES + 1),
            shape((heads, 2 * HD, tok), BF16), shape((heads, 8, tok), F32),
        ),
        [
            pltpu.VMEM((chunks, CH, tok), F32), pltpu.VMEM((chunks, CH, tok), F32),
            pltpu.VMEM((chunks, CH, tok), BF16),
            pltpu.VMEM((chunks - tok // CH, 2 * HD, CH), F32), pltpu.VMEM((2, 8, tok), F32),
        ],
        24, 10**10, (qz, dz, mid, ahead, behind, other0, other1),
    )
    low0, low1 = call(
        combine_kernel, "combine", (shape((tok, 2 * HD), BF16),) * 2, [], 4, 10**6,
        (mine, partnered(lent)),
    )
    back, forth = swap(low0, 0), swap(low1, 1)
    dqt, own = call(
        functools.partial(finish_kernel, heads, tok), "finish",
        (shape((heads, HD, tok), BF16), shape((tok, 2 * HD), F32)),
        [pltpu.VMEM((2 * HD, tok), F32)],
        8, 3 * 10**9, (kt, *g, eown, w, r, low0),
    )
    keep, send = call(
        functools.partial(settle_kernel, tok // 2), "settle",
        (shape((tok // 2, 2 * HD), F32),) * 2, [], 4, 10**6, (own, back, forth),
    )
    theirs = partnered(send)
    (dquery,) = call(
        functools.partial(tail_kernel, heads, tok), "tail",
        (shape((tok, width), BF16),), [], 8, 10**9, (dqt, send),
    )
    return dquery[None, None], (keep + theirs)[None, None]


def solution(mesh):
    placed = (
        P("lat", "lon", None, "head"),
        P("lat", "lon", None, None),
        P("lat", "lon", None, "head"),
    )
    return jax.shard_map(
        local,
        mesh=mesh,
        in_specs=placed,
        out_specs=(P("lat", "lon", None, "head"), P("lat", "lon", "head", None)),
        check_vma=False,
    )
```
